1024 devices in a mesh: ctx: 16 (over y, core), uly: 64 (over x, z).
Axes of the slice: x: 8, y: 8, z: 8, core: 2. Of those that a mesh axis runs over, the one named last changes fastest.
Arguments:
- queries: bfloat16 [98304, 4096], P(('ctx', 'uly')), may hold values from -6 to 6
- keys: bfloat16 [98304, 4096], P(('ctx', 'uly')), may hold values from -6 to 6
- values: bfloat16 [98304, 4096], P(('ctx', 'uly')), may hold values from -6 to 6
- doc_ids: int32 [98304], P(('ctx', 'uly')), may hold values from 0 to 31, never falling along the last dimension, each value on 1 to 12288 neighbouring positions
- decay_rate: float32 [64], P('uly'), may hold values from 8.138021e-06 to 0.05
- norm_gain: float32 [4096], replicated, may hold values from 0.1 to 1.9
Outputs:
- attended: bfloat16 [98304, 4096], P(('ctx', 'uly'))
The draws below stay inside these ranges and needn't reach their ends.
Inputs may be any that keep to these rules, and one draw needn't show every extreme that they name: doc_ids never fall along the sequence; every document has 1 to 12288 tokens and one has exactly that many.
All inputs are finite; a program needn't handle non-finite values.
Results may differ from the reference program's by a relative error of at most 0.0034.
Values may be sent and summed in bfloat16 or wider, within the bound.
A program may use at most 32 MiB of HBM per device.

```python
import math
import jax
import jax.numpy as jnp
import numpy as np
from jax import lax

H = 64
HD = 64
BLK = 256
L_CTX = 6144
TOKENS = 98304
DOCS = 32


def levels(own_key, extent, cuts, smallest, top_value):
    loudness, own = 1.0, jax.random.fold_in(own_key, 6)
    for dim, blocks in cuts:
        steps = jnp.exp(jax.random.uniform(jax.random.fold_in(own, dim), (blocks,), jnp.float32, smallest / len(cuts), top_value / len(cuts)))
        loudness = loudness * jnp.repeat(steps, extent[dim] // blocks).reshape([-1 if axis == dim else 1 for axis in range(len(extent))])
    return loudness


def split_up(count, total, reach, slope):
    portions = [(1 << 20) // math.isqrt(grade ** slope) + 1 for grade in range(2, count + 1)]
    rest, holding = total - reach - (count - 1), [1] * (count - 1)
    while rest > 0:
        free = [i for i in range(count - 1) if holding[i] < reach]
        pool, left = sum([portions[i] for i in free]), rest
        for i in free:
            extra = min(reach - holding[i], max(1, left * portions[i] // pool), rest)
            holding[i] = holding[i] + extra
            rest = rest - extra
    return np.array([reach] + holding)


def ragged(stream_key, count, total, limit, lean):
    if count == 2:
        one = jax.random.randint(stream_key, (), max(1, total - limit), min(limit, total - 1) + 1)
        return jnp.stack([one, total - one])
    tallies = jnp.asarray(split_up(count, total, limit, lean), jnp.int32)
    pairs = (count - 1) // 2
    giver, taker = tallies[1:1 + 2 * pairs:2], tallies[2:2 + 2 * pairs:2]
    slack = jnp.minimum(giver - 1, limit - taker)
    passed = jax.random.randint(jax.random.fold_in(stream_key, 1), (pairs,), 0, 1 << 20) % (slack + 1)
    tallies = tallies.at[1:1 + 2 * pairs:2].set(giver - passed).at[2:2 + 2 * pairs:2].set(taker + passed)
    return tallies[jax.random.permutation(jax.random.fold_in(stream_key, 2), count)]


def gaussian(own_key, extent, scale, bound, cuts=(), held_as=jnp.bfloat16):
    values = scale * jax.random.normal(own_key, extent, jnp.float32)
    if cuts:
        values = values * levels(own_key, extent, cuts, -0.22, 0.18)
    return jnp.clip(values, -bound, bound).astype(held_as)


def setup_inputs(seed: int = 0) -> dict:
    key_of = jax.random.split(jax.random.key(seed), 7)
    queries = gaussian(key_of[0], (TOKENS, H * HD), 1.0, 6.0, ((0, 1024),))
    keys = gaussian(key_of[1], (TOKENS, H * HD), 1.0, 6.0, ((0, 1024),))
    values = gaussian(key_of[2], (TOKENS, H * HD), 1.0, 6.0, ((0, 1024),))
    doc_ids = jnp.searchsorted(jnp.cumsum(ragged(key_of[3], DOCS, TOKENS, 2 * L_CTX, 2)), jnp.arange(TOKENS), side="right").astype(jnp.int32)
    decay_rate = jnp.clip(jnp.exp(math.log(0.05) - 8.723231 * jax.random.uniform(key_of[4], (H,), jnp.float32) ** levels(key_of[4], (H,), ((0, 64),), -0.2, 0.2)), 8.138021257764194e-06, 0.05)
    norm_gain = jnp.clip(1.0 + 0.18 * jax.random.normal(key_of[5], (H * HD,), jnp.float32), 0.1, 1.9)
    return dict(queries=queries, keys=keys, values=values, doc_ids=doc_ids, decay_rate=decay_rate, norm_gain=norm_gain)


def state_pass(keys3, values3, ids, rate, blk, start_state, start_last):
    length, heads, width = keys3.shape
    count = length // blk
    kblocks = keys3.reshape(count, blk, heads, width)
    vblocks = values3.reshape(count, blk, heads, width)
    iblocks = ids.reshape(count, blk)
    position = jnp.arange(blk).astype(jnp.float32)

    def advance(carry, pieces):
        state, last = carry
        kblock, vblock, iblock = pieces
        endid = iblock[blk - 1]
        keep = jnp.where(endid == last, jnp.exp(-rate * blk), jnp.float32(0.0))
        weights = jnp.where((iblock == endid)[None, :], jnp.exp(-rate[:, None] * (blk - 1 - position)[None, :]), jnp.float32(0.0))
        scaled = kblock.astype(jnp.float32) * jnp.transpose(weights)[:, :, None]
        fresh = jnp.einsum('shd,she->hde', scaled, vblock.astype(jnp.float32), precision=lax.Precision.HIGHEST)
        return ((keep[:, None, None] * state + fresh, endid), (state, last))
    final, entries = lax.scan(advance, (start_state, start_last), (kblocks, vblocks, iblocks))
    return (final, entries)

def block_output(qblock, kblock, vblock, iblock, state, last, rate):
    blk = qblock.shape[0]
    position = jnp.arange(blk).astype(jnp.float32)
    q32 = qblock.astype(jnp.float32)
    scores = jnp.einsum('thd,shd->hts', q32, kblock.astype(jnp.float32))
    diff = position[:, None] - position[None, :]
    mask = (diff >= 0) & (iblock[:, None] == iblock[None, :])
    weight = jnp.where(mask[None], jnp.exp(-rate[:, None, None] * jnp.maximum(diff, 0.0)[None]), jnp.float32(0.0))
    probs = (scores * weight).astype(jnp.bfloat16)
    intra = jnp.einsum('hts,shd->thd', probs.astype(jnp.float32), vblock.astype(jnp.float32))
    factor = jnp.exp(-rate[None, :] * (position + 1.0)[:, None]) * (iblock == last).astype(jnp.float32)[:, None]
    inter = jnp.einsum('thd,hde->the', q32, state, precision=lax.Precision.HIGHEST) * factor[:, :, None]
    return intra + inter

def all_outputs(q3, k3, v3, ids, rate, blk, entries):
    length, heads, width = q3.shape
    count = length // blk
    states, lasts = entries

    def one(pieces):
        qblock, kblock, vblock, iblock, state, last = pieces
        return block_output(qblock, kblock, vblock, iblock, state, last, rate)
    out = lax.map(one, (q3.reshape(count, blk, heads, width), k3.reshape(count, blk, heads, width), v3.reshape(count, blk, heads, width), ids.reshape(count, blk), states, lasts))
    return out.reshape(length, heads, width)

def token_norm(raw, gain):
    flat = raw.reshape(raw.shape[0], raw.shape[1] * raw.shape[2])
    meansq = lax.optimization_barrier(jnp.mean(flat * flat, axis=1, keepdims=True))
    return (flat * lax.rsqrt(meansq + 1e-06) * gain[None, :]).astype(jnp.bfloat16)

def reference(queries, keys, values, doc_ids, decay_rate, norm_gain):
    q3 = queries.reshape(TOKENS, H, HD)
    k3 = keys.reshape(TOKENS, H, HD)
    v3 = values.reshape(TOKENS, H, HD)
    zero_state = jnp.zeros((H, HD, HD), jnp.float32)
    final, entries = state_pass(k3, v3, doc_ids, decay_rate, BLK, zero_state, jnp.int32(-1))
    raw = all_outputs(q3, k3, v3, doc_ids, decay_rate, BLK, entries)
    return token_norm(raw, norm_gain)
```

```python
import functools
import math
import jax
import jax.numpy as jnp
from jax import lax
from jax.experimental import pallas as pl
from jax.experimental.pallas import tpu as pltpu
from jax.sharding import PartitionSpec as P

HD = 64
PAIR = 2 * HD
F32 = jnp.float32
BF16 = jnp.bfloat16
MESH = pl.DeviceIdType.MESH
CONTRACT_ROWS = (((0,), (0,)), ((), ()))
CONTRACT_LANES = (((1,), (1,)), ((), ()))
PLAIN = (((1,), (0,)), ((), ()))
FAR = -1e30


def dot(a, b, dims):
    return lax.dot_general(a, b, dims, preferred_element_type=F32)


def kernel(nx, nz, nctx, tok, q_hbm, k_hbm, v_hbm, ids_ref, rate_ref, gain_ref, out_ref,
           q_ref, k_ref, v_ref, info, negdiff, doc, raw, sumsq,
           s_send, s_recv, line, t_recv, u_buf, c_send, c1_recv, c2_recv, o_send, o_recv,
           p_send, p_recv, prev_row,
           load_sem, iz_s, iz_r, ix_s, ix_r, s_s, s_r, t_s, t_r, c_s, c_r, o_s, o_r, p_s, p_r):
    n = nx * nz
    chunks = nx // 2
    rx = HD // nx
    slab = nz * tok
    ctx = lax.axis_index("ctx")
    me = lax.axis_index("uly")
    x, z = me // nz, me % nz

    loads = [pltpu.make_async_copy(a, b, load_sem.at[i])
             for i, (a, b) in enumerate(((k_hbm, k_ref), (v_hbm, v_ref), (q_hbm, q_ref)))]
    for load in loads:
        load.start()
    barrier = pltpu.get_barrier_semaphore()

    def on_line(off):
        return (z + off) % nz

    def on_column(off):
        return (x + off) % nx

    def dev(xx, zz):
        return (ctx, xx * nz + zz)

    def later(steps):
        return ((ctx + steps + nctx) % nctx, me)

    def greet_z(off, _):
        pl.semaphore_signal(barrier, inc=1, device_id=dev(x, on_line(off)), device_id_type=MESH)
        return 0

    def greet_x(off, _):
        pl.semaphore_signal(barrier, inc=1, device_id=dev(on_column(off), z), device_id_type=MESH)
        return 0

    lax.fori_loop(1, nz, greet_z, 0)
    lax.fori_loop(1, nx, greet_x, 0)
    for steps in (1, 2, -1, -2):
        pl.semaphore_signal(barrier, inc=1, device_id=later(steps), device_id_type=MESH)

    ids = ids_ref[...].astype(F32)
    last = jnp.max(ids, axis=1, keepdims=True)
    sub = lax.broadcasted_iota(jnp.int32, (8, PAIR), 0)
    info[me] = jnp.where(sub < 4, jnp.full((8, PAIR), rate_ref[0], F32),
                         jnp.broadcast_to(last, (8, PAIR)))
    t_at = lax.broadcasted_iota(jnp.int32, (tok, tok), 0)
    s_at = lax.broadcasted_iota(jnp.int32, (tok, tok), 1)
    ids_all = jnp.broadcast_to(ids, (tok, tok))
    column = jnp.sum(jnp.where(t_at == s_at, ids_all, 0.0), axis=1, keepdims=True)
    negdiff[...] = jnp.where((t_at >= s_at) & (column == ids_all), (s_at - t_at).astype(F32), FAR)
    doc[...] = jnp.broadcast_to(column, (tok, PAIR))
    sumsq[...] = jnp.zeros_like(sumsq)
    pl.semaphore_wait(barrier, nz + nx - 2 + 4)

    def info_z(to, frm):
        return pltpu.make_async_remote_copy(info.at[frm], info.at[frm], iz_s.at[to % nz], iz_r.at[frm % nz],
                                            device_id=(ctx, to), device_id_type=MESH)

    def info_x(xto, xfrm):
        rows = info.at[pl.ds(xfrm * nz, nz)]
        return pltpu.make_async_remote_copy(rows, rows, ix_s.at[xto], ix_r.at[xfrm],
                                            device_id=dev(xto, z), device_id_type=MESH)

    def loop_z(body):
        def step(off, _):
            body(on_line(off))
            return 0
        lax.fori_loop(1, nz, step, 0)

    def loop_x(body):
        def step(off, _):
            body(on_column(off))
            return 0
        lax.fori_loop(1, nx, step, 0)

    loop_z(lambda zz: info_z(x * nz + zz, me).start())
    loop_z(lambda zz: info_z(me, x * nz + zz).wait_recv())
    loop_x(lambda xx: info_x(xx, x).start())
    for load in loads:
        load.wait()
    loop_x(lambda xx: info_x(x, xx).wait_recv())

    low = lax.broadcasted_iota(jnp.int32, (1, PAIR), 1) < HD
    mask_low = jnp.where(low, 1.0, 0.0)
    keep_low = mask_low.astype(BF16)
    keep_high = (1.0 - mask_low).astype(BF16)

    def pair_rate(pair):
        return jnp.where(low, info[2 * pair, 0:1, :], info[2 * pair + 1, 0:1, :])

    def last_of(j):
        return info[j, 4:5, :]

    def pair_columns(pair):
        return pl.ds(pl.multiple_of(pair * PAIR, PAIR), PAIR)

    def join(big, rows):
        return jnp.where(low, big[:rows], big[rows:])

    after = (tok - 1 - lax.broadcasted_iota(jnp.int32, (tok, PAIR), 0)).astype(F32)
    after = jnp.where(doc[...] == last_of(me), -after, FAR)

    def end_state(pair):
        kp = k_ref[:, pair_columns(pair)].astype(F32) * jnp.exp(after * pair_rate(pair))
        vp = v_ref[:, pair_columns(pair)]
        high = kp.astype(BF16)
        rest = (kp - high.astype(F32)).astype(BF16)
        both = dot(jnp.concatenate([high, rest], 0), jnp.concatenate([vp, vp], 0), CONTRACT_ROWS)
        return join(both, HD).astype(BF16)

    def send_state(c, to, frm):
        return pltpu.make_async_remote_copy(s_send.at[c, to], s_recv.at[c, frm], s_s.at[c, to], s_r.at[c, frm],
                                            device_id=dev(x, to), device_id_type=MESH)

    for c in range(chunks):
        def state_out(zz, c=c):
            s_send[c, zz] = end_state(zz * chunks + c)
            send_state(c, zz, z).start()
        loop_z(state_out)
        s_recv[c, z] = end_state(z * chunks + c)

    def intra(pair, _):
        columns = pair_columns(pair)
        q2 = q_ref[:, columns]
        qq = jnp.concatenate([q2 * keep_low, q2 * keep_high], 0)
        scores = dot(qq, k_ref[:, columns], CONTRACT_LANES)
        gaps = negdiff[...]
        weight = jnp.concatenate([jnp.exp(gaps * info[2 * pair, 0:1, :tok]),
                                  jnp.exp(gaps * info[2 * pair + 1, 0:1, :tok])], 0)
        probs = (scores * weight).astype(BF16)
        raw[:, columns] = join(dot(probs, v_ref[:, columns], PLAIN), tok)
        return 0

    def send_total(c, to, frm):
        return pltpu.make_async_remote_copy(line.at[nz, c, pl.ds(pl.multiple_of(to * rx, rx), rx)], t_recv.at[c, frm],
                                            t_s.at[c, to], t_r.at[c, frm],
                                            device_id=dev(to, z), device_id_type=MESH)

    def scan_line(c):
        loop_z(lambda zz: send_state(c, z, zz).wait_recv())
        decay = jnp.exp(-float(tok) * pair_rate(z * chunks + c))
        total = jnp.zeros((HD, PAIR), F32)
        for zz in range(nz):
            line[zz, c] = total
            state = s_recv[c, zz].astype(F32)
            if zz:
                here = last_of(x * nz + zz)
                state = state + jnp.where(here == last_of(x * nz + zz - 1), decay, 0.0) * total
            total = state
        line[nz, c] = total
        t_recv[c, x] = line[nz, c, pl.ds(pl.multiple_of(x * rx, rx), rx)]
        loop_x(lambda xx: send_total(c, xx, x).start())

    def send_slice(c, steps):
        land, i = ((c1_recv, 0), (c2_recv, 1))[steps - 1]
        return pltpu.make_async_remote_copy(c_send.at[c], land.at[c], c_s.at[c, i], c_r.at[c, i],
                                            device_id=later(steps), device_id_type=MESH)

    def scan_lines(c):
        loop_x(lambda xx: send_total(c, x, xx).wait_recv())
        decay = jnp.exp(-float(slab) * pair_rate(z * chunks + c))
        total = jnp.zeros((rx, PAIR), F32)
        for xx in range(nx):
            u_buf[c, xx] = total
            state = t_recv[c, xx]
            if xx:
                linked = last_of(xx * nz + nz - 1) == last_of(xx * nz - 1)
                state = state + jnp.where(linked, decay, 0.0) * total
            total = state
        c_send[c, 0:rx] = total
        c_send[c, rx:rx + 8] = jnp.broadcast_to(last_of(n - 1), (8, PAIR))
        send_slice(c, 1).start()
        send_slice(c, 2).start()

    def send_carry(c, to, frm):
        return pltpu.make_async_remote_copy(o_send.at[c, to], o_recv.at[c, frm], o_s.at[c, to], o_r.at[c, frm],
                                            device_id=dev(to, z), device_id_type=MESH)

    def carry_lines(c):
        send_slice(c, 1).wait_recv()
        send_slice(c, 2).wait_recv()
        rate = pair_rate(z * chunks + c)
        one, two = c1_recv[c, 0:rx], c2_recv[c, 0:rx]
        last_one, last_two = c1_recv[c, rx:rx + 1], c2_recv[c, rx:rx + 1]
        reach = jnp.where((ctx >= 2) & (last_one == last_two), jnp.exp(-float(slab * nx) * rate), 0.0)
        carry = jnp.where(ctx >= 1, one + reach * two, 0.0)
        before = jnp.where(ctx >= 1, last_one, -1.0)
        if c == 0:
            prev_row[...] = jnp.broadcast_to(before, (8, PAIR))
        for xx in range(nx):
            value = u_buf[c, xx]
            if xx:
                linked = last_of(xx * nz - 1) == before
                value = value + jnp.where(linked, jnp.exp(-float(slab * xx) * rate), 0.0) * carry
            else:
                value = value + carry
            o_send[c, xx] = value
        o_recv[c, x] = o_send[c, x]
        loop_x(lambda xx: send_carry(c, xx, x).start())

    def send_prefix(c, to, frm):
        return pltpu.make_async_remote_copy(p_send.at[c, to], p_recv.at[c, frm], p_s.at[c, to], p_r.at[c, frm],
                                            device_id=dev(x, to), device_id_type=MESH)

    def before_line():
        return jnp.where(x == 0, prev_row[0:1], last_of((me - z + n - 1) % n))

    def prefixes(c):
        loop_x(lambda xx: send_carry(c, x, xx).wait_recv())
        rate = pair_rate(z * chunks + c)
        before = before_line()

        def prefix(zz):
            linked = (zz == 0) | (last_of((x * nz + zz + n - 1) % n) == before)
            reach = jnp.where(linked, jnp.exp(-float(tok) * zz.astype(F32) * rate), 0.0)
            return (line[zz, c] + reach * o_recv[c].reshape(HD, PAIR)).astype(BF16)

        def prefix_out(zz):
            p_send[c, zz] = prefix(zz)
            send_prefix(c, zz, z).start()

        loop_z(prefix_out)
        p_recv[c, z] = prefix(z)

    upto = -(1 + lax.broadcasted_iota(jnp.int32, (tok, PAIR), 0)).astype(F32)

    def finish(c):
        before = jnp.where(z == 0, before_line(), last_of((me + n - 1) % n))
        gaps = jnp.where(doc[...] == before, upto, FAR)

        def add(zz):
            pair = zz * chunks + c
            columns = pair_columns(pair)
            state = p_recv[c, zz]
            wide = jnp.concatenate([state * keep_low, state * keep_high], 0)
            inter = dot(q_ref[:, columns], wide, PLAIN)
            value = raw[:, columns] + inter * jnp.exp(gaps * pair_rate(pair))
            raw[:, columns] = value
            sumsq[...] += value * value

        add(z)

        def arrived(zz):
            send_prefix(c, z, zz).wait_recv()
            add(zz)
        loop_z(arrived)

    pairs = n // 2
    steps = chunks + 5
    done = 0
    for step in range(steps):
        want = min(pairs, (pairs * (step + 1) + 5) // 6)
        if want > done:
            lax.fori_loop(done, want, intra, 0)
            done = want
        if step < chunks:
            scan_line(step)
        if 0 <= step - 2 < chunks:
            scan_lines(step - 2)
        if 0 <= step - 3 < chunks:
            carry_lines(step - 3)
        if 0 <= step - 5 < chunks:
            prefixes(step - 5)
    for c in range(chunks):
        finish(c)

    width = n * HD
    mean = jnp.sum(sumsq[...], axis=1, keepdims=True) * (1.0 / width)
    scale = jnp.broadcast_to(lax.rsqrt(mean + 1e-6), (tok, PAIR))

    def write(pair, _):
        columns = pair_columns(pair)
        out_ref[:, columns] = (raw[:, columns] * scale * gain_ref[0:1, columns]).astype(BF16)
        return 0
    lax.fori_loop(0, pairs, write, 0)

    loop_z(lambda zz: info_z(x * nz + zz, me).wait_send())
    loop_x(lambda xx: info_x(xx, x).wait_send())
    for c in range(chunks):
        loop_z(lambda zz: send_state(c, zz, z).wait_send())
        loop_x(lambda xx: send_total(c, xx, x).wait_send())
        send_slice(c, 1).wait_send()
        send_slice(c, 2).wait_send()
        loop_x(lambda xx: send_carry(c, xx, x).wait_send())
        loop_z(lambda zz: send_prefix(c, zz, z).wait_send())


def solution(mesh, nz=None):
    nctx, n = mesh.shape["ctx"], mesh.shape["uly"]
    nz = nz or math.isqrt(n)
    nx = n // nz
    chunks, rx = nx // 2, HD // nx

    def local(queries, keys, values, doc_ids, decay_rate, norm_gain):
        tok, width = queries.shape
        vmem = pl.BlockSpec(memory_space=pltpu.VMEM)
        anywhere = pl.BlockSpec(memory_space=pl.ANY)
        sem = pltpu.SemaphoreType.DMA
        return pl.pallas_call(
            functools.partial(kernel, nx, nz, nctx, tok),
            out_shape=jax.ShapeDtypeStruct((tok, width), BF16),
            in_specs=[anywhere, anywhere, anywhere, vmem, pl.BlockSpec(memory_space=pltpu.SMEM), vmem],
            out_specs=vmem,
            scratch_shapes=[
                pltpu.VMEM((tok, width), BF16),
                pltpu.VMEM((tok, width), BF16),
                pltpu.VMEM((tok, width), BF16),
                pltpu.VMEM((n, 8, PAIR), F32),
                pltpu.VMEM((tok, tok), F32),
                pltpu.VMEM((tok, PAIR), F32),
                pltpu.VMEM((tok, width), F32),
                pltpu.VMEM((tok, PAIR), F32),
                pltpu.VMEM((chunks, nz, HD, PAIR), BF16),
                pltpu.VMEM((chunks, nz, HD, PAIR), BF16),
                pltpu.VMEM((nz + 1, chunks, HD, PAIR), F32),
                pltpu.VMEM((chunks, nx, rx, PAIR), F32),
                pltpu.VMEM((chunks, nx, rx, PAIR), F32),
                pltpu.VMEM((chunks, rx + 8, PAIR), F32),
                pltpu.VMEM((chunks, rx + 8, PAIR), F32),
                pltpu.VMEM((chunks, rx + 8, PAIR), F32),
                pltpu.VMEM((chunks, nx, rx, PAIR), F32),
                pltpu.VMEM((chunks, nx, rx, PAIR), F32),
                pltpu.VMEM((chunks, nz, HD, PAIR), BF16),
                pltpu.VMEM((chunks, nz, HD, PAIR), BF16),
                pltpu.VMEM((8, PAIR), F32),
                sem((3,)),
                sem((nz,)), sem((nz,)), sem((nx,)), sem((nx,)),
                sem((chunks, nz)), sem((chunks, nz)),
                sem((chunks, nx)), sem((chunks, nx)),
                sem((chunks, 2)), sem((chunks, 2)),
                sem((chunks, nx)), sem((chunks, nx)),
                sem((chunks, nz)), sem((chunks, nz)),
            ],
            compiler_params=pltpu.CompilerParams(collective_id=0, has_side_effects=True,
                                                 vmem_limit_bytes=48 * 1024 * 1024),
        )(queries, keys, values, doc_ids.reshape(1, tok), decay_rate, norm_gain.reshape(1, width))

    rows = P(("ctx", "uly"), None)
    return jax.shard_map(local, mesh=mesh,
                         in_specs=(rows, rows, rows, P(("ctx", "uly")), P("uly"), P()),
                         out_specs=rows, check_vma=False)
```

```python
import functools
import math
import jax
import jax.numpy as jnp
from jax import lax
from jax.experimental import pallas as pl
from jax.experimental.pallas import tpu as pltpu
from jax.sharding import PartitionSpec as P

HD = 64
PAIR = 2 * HD
F32 = jnp.float32
BF16 = jnp.bfloat16
MESH = pl.DeviceIdType.MESH
CONTRACT_ROWS = (((0,), (0,)), ((), ()))
CONTRACT_LANES = (((1,), (1,)), ((), ()))
PLAIN = (((1,), (0,)), ((), ()))
FAR = -1e30


def dot(a, b, dims):
    return lax.dot_general(a, b, dims, preferred_element_type=F32)


def kernel(nx, nz, nctx, tok, q_hbm, k_hbm, v_hbm, ids_hbm, gain_hbm, rate_ref, out_ref,
           ids_ref, gain_ref, q_ref, k_ref, v_ref, k_turned, scores, info, negdiff, doc, raw, sumsq,
           s_send, s_recv, line, t_recv, u_buf, c_send, c1_recv, c2_recv, o_send, o_recv,
           p_send, p_recv, prev_row,
           load_sem, iz_s, iz_r, ix_s, ix_r, s_s, s_r, t_s, t_r, c_s, c_r, o_s, o_r, p_s, p_r):
    n = nx * nz
    chunks = nx // 2
    rx = HD // nx
    slab = nz * tok
    ctx = lax.axis_index("ctx")
    me = lax.axis_index("uly")
    x, z = me // nz, me % nz

    loads = [pltpu.make_async_copy(a, b, load_sem.at[i])
             for i, (a, b) in enumerate(((ids_hbm, ids_ref), (k_hbm, k_ref), (v_hbm, v_ref), (q_hbm, q_ref), (gain_hbm, gain_ref)))]
    barrier = pltpu.get_barrier_semaphore()

    def on_line(off):
        return (z + off) % nz

    def on_column(off):
        return (x + off) % nx

    def dev(xx, zz):
        return (ctx, xx * nz + zz)

    def later(steps):
        return ((ctx + steps + nctx) % nctx, me)

    def greet_z(off, _):
        pl.semaphore_signal(barrier, inc=1, device_id=dev(x, on_line(off)), device_id_type=MESH)
        return 0

    def greet_x(off, _):
        pl.semaphore_signal(barrier, inc=1, device_id=dev(on_column(off), z), device_id_type=MESH)
        return 0

    lax.fori_loop(1, nz, greet_z, 0)
    lax.fori_loop(1, nx, greet_x, 0)
    for steps in (1, 2, -1, -2):
        pl.semaphore_signal(barrier, inc=1, device_id=later(steps), device_id_type=MESH)
    for load in loads:
        load.start()

    loads[0].wait()
    ids = ids_ref[...].astype(F32)
    last = jnp.max(ids, axis=1, keepdims=True)
    info[me] = jnp.where(lax.broadcasted_iota(jnp.int32, (2, PAIR), 0) < 1, jnp.full((2, PAIR), rate_ref[0], F32),
                         jnp.broadcast_to(last, (2, PAIR)))
    t_at = lax.broadcasted_iota(jnp.int32, (tok, tok), 0)
    s_at = lax.broadcasted_iota(jnp.int32, (tok, tok), 1)
    ids_all = jnp.broadcast_to(ids, (tok, tok))
    column = jnp.sum(jnp.where(t_at == s_at, ids_all, 0.0), axis=1, keepdims=True)
    negdiff[...] = jnp.where((t_at >= s_at) & (column == ids_all), (s_at - t_at).astype(F32), FAR)
    doc[...] = jnp.broadcast_to(column, (tok, PAIR))
    sumsq[...] = jnp.zeros_like(sumsq)
    pl.semaphore_wait(barrier, nz + nx - 2 + 4)

    def info_z(to, frm):
        return pltpu.make_async_remote_copy(info.at[frm], info.at[frm], iz_s.at[to % nz], iz_r.at[frm % nz],
                                            device_id=(ctx, to), device_id_type=MESH)

    def info_x(xto, xfrm):
        rows = info.at[pl.ds(xfrm * nz, nz)]
        return pltpu.make_async_remote_copy(rows, rows, ix_s.at[xto], ix_r.at[xfrm],
                                            device_id=dev(xto, z), device_id_type=MESH)

    def loop_z(body):
        def step(off, _):
            body(on_line(off))
            return 0
        lax.fori_loop(1, nz, step, 0)

    def loop_x(body):
        def step(off, _):
            body(on_column(off))
            return 0
        lax.fori_loop(1, nx, step, 0)

    low = lax.broadcasted_iota(jnp.int32, (1, PAIR), 1) < HD
    mask_low = jnp.where(low, 1.0, 0.0)
    keep_low = mask_low.astype(BF16)
    keep_high = (1.0 - mask_low).astype(BF16)

    def pair_columns(pair):
        return pl.ds(pl.multiple_of(pair * PAIR, PAIR), PAIR)

    pairs = n // 2

    def over_pairs(first, end, width, body):
        def step(i, _):
            for j in range(width):
                body(first + i * width + j)
            return 0
        lax.fori_loop(0, (end - first) // width, step, 0)

    def turn(pair):
        k_turned[pair] = k_ref[:, pair_columns(pair)].astype(F32).T

    def score(pair):
        q2 = q_ref[:, pair_columns(pair)]
        qq = jnp.concatenate([q2 * keep_low, q2 * keep_high], 0)
        scores[pair] = dot(qq, k_ref[:, pair_columns(pair)], CONTRACT_LANES)

    loop_z(lambda zz: info_z(x * nz + zz, me).start())
    loads[1].wait()
    over_pairs(0, pairs, 4, turn)
    loop_z(lambda zz: info_z(me, x * nz + zz).wait_recv())
    loop_x(lambda xx: info_x(xx, x).start())
    for load in loads[2:]:
        load.wait()
    over_pairs(0, pairs, 4, score)
    loop_x(lambda xx: info_x(x, xx).wait_recv())

    def pair_rate(pair):
        return jnp.where(low, info[2 * pair, 0:1, :], info[2 * pair + 1, 0:1, :])

    def last_of(j):
        return info[j, 1:2, :]

    def join(big, rows):
        return jnp.where(low, big[:rows], big[rows:])

    after = (tok - 1 - lax.broadcasted_iota(jnp.int32, (1, tok), 1)).astype(F32)
    after = jnp.where(ids == last, -after, FAR)

    def end_state(pair):
        turned = k_turned[pair]
        kp = jnp.concatenate([turned[:HD] * jnp.exp(after * info[2 * pair, 0:1, :tok]),
                              turned[HD:] * jnp.exp(after * info[2 * pair + 1, 0:1, :tok])], 0)
        vp = v_ref[:, pair_columns(pair)]
        high = kp.astype(BF16)
        rest = (kp - high.astype(F32)).astype(BF16)
        return join(dot(high, vp, PLAIN) + dot(rest, vp, PLAIN), HD).astype(BF16)

    def send_state(c, to, frm):
        return pltpu.make_async_remote_copy(s_send.at[c, to], s_recv.at[c, frm], s_s.at[c, to], s_r.at[c, frm],
                                            device_id=dev(x, to), device_id_type=MESH)

    for c in range(chunks):
        for off in range(1, nz):
            s_send[c, on_line(off)] = end_state(on_line(off) * chunks + c)
        loop_z(lambda zz: send_state(c, zz, z).start())
        s_recv[c, z] = end_state(z * chunks + c)

    def intra(pair):
        gaps = negdiff[...]
        weight = jnp.concatenate([jnp.exp(gaps * info[2 * pair, 0:1, :tok]),
                                  jnp.exp(gaps * info[2 * pair + 1, 0:1, :tok])], 0)
        probs = (scores[pair] * weight).astype(BF16)
        raw[:, pair_columns(pair)] = join(dot(probs, v_ref[:, pair_columns(pair)], PLAIN), tok)

    def send_total(c, to, frm):
        return pltpu.make_async_remote_copy(line.at[nz, c, pl.ds(pl.multiple_of(to * rx, rx), rx)], t_recv.at[c, frm],
                                            t_s.at[c, to], t_r.at[c, frm],
                                            device_id=dev(to, z), device_id_type=MESH)

    def scan_line(c):
        loop_z(lambda zz: send_state(c, z, zz).wait_recv())
        decay = jnp.exp(-float(tok) * pair_rate(z * chunks + c))
        total = jnp.zeros((HD, PAIR), F32)
        for zz in range(nz):
            line[zz, c] = total
            state = s_recv[c, zz].astype(F32)
            if zz:
                here = last_of(x * nz + zz)
                state = state + jnp.where(here == last_of(x * nz + zz - 1), decay, 0.0) * total
            total = state
        line[nz, c] = total
        t_recv[c, x] = line[nz, c, pl.ds(pl.multiple_of(x * rx, rx), rx)]
        loop_x(lambda xx: send_total(c, xx, x).start())

    def send_slice(c, steps):
        land, i = ((c1_recv, 0), (c2_recv, 1))[steps - 1]
        return pltpu.make_async_remote_copy(c_send.at[c], land.at[c], c_s.at[c, i], c_r.at[c, i],
                                            device_id=later(steps), device_id_type=MESH)

    def scan_lines(c):
        loop_x(lambda xx: send_total(c, x, xx).wait_recv())
        decay = jnp.exp(-float(slab) * pair_rate(z * chunks + c))
        total = jnp.zeros((rx, PAIR), F32)
        for xx in range(nx):
            u_buf[c, xx] = total
            state = t_recv[c, xx]
            if xx:
                linked = last_of(xx * nz + nz - 1) == last_of(xx * nz - 1)
                state = state + jnp.where(linked, decay, 0.0) * total
            total = state
        c_send[c, 0:rx] = total
        c_send[c, rx:rx + 8] = jnp.broadcast_to(last_of(n - 1), (8, PAIR))
        send_slice(c, 1).start()
        send_slice(c, 2).start()

    def send_carry(c, to, frm):
        return pltpu.make_async_remote_copy(o_send.at[c, to], o_recv.at[c, frm], o_s.at[c, to], o_r.at[c, frm],
                                            device_id=dev(to, z), device_id_type=MESH)

    def carry_lines(c):
        send_slice(c, 1).wait_recv()
        send_slice(c, 2).wait_recv()
        rate = pair_rate(z * chunks + c)
        one, two = c1_recv[c, 0:rx], c2_recv[c, 0:rx]
        last_one, last_two = c1_recv[c, rx:rx + 1], c2_recv[c, rx:rx + 1]
        reach = jnp.where((ctx >= 2) & (last_one == last_two), jnp.exp(-float(slab * nx) * rate), 0.0)
        carry = jnp.where(ctx >= 1, one + reach * two, 0.0)
        before = jnp.where(ctx >= 1, last_one, -1.0)
        if c == 0:
            prev_row[...] = jnp.broadcast_to(before, (8, PAIR))
        for xx in range(nx):
            value = u_buf[c, xx]
            if xx:
                linked = last_of(xx * nz - 1) == before
                value = value + jnp.where(linked, jnp.exp(-float(slab * xx) * rate), 0.0) * carry
            else:
                value = value + carry
            o_send[c, xx] = value
        o_recv[c, x] = o_send[c, x]
        loop_x(lambda xx: send_carry(c, xx, x).start())

    def send_prefix(c, to, frm):
        return pltpu.make_async_remote_copy(p_send.at[c, to], p_recv.at[c, frm], p_s.at[c, to], p_r.at[c, frm],
                                            device_id=dev(x, to), device_id_type=MESH)

    def before_line():
        return jnp.where(x == 0, prev_row[0:1], last_of((me - z + n - 1) % n))

    def prefixes(c):
        loop_x(lambda xx: send_carry(c, x, xx).wait_recv())
        rate = pair_rate(z * chunks + c)
        before = before_line()

        def prefix(zz):
            linked = (zz == 0) | (last_of((x * nz + zz + n - 1) % n) == before)
            reach = jnp.where(linked, jnp.exp(-float(tok) * zz.astype(F32) * rate), 0.0)
            return (line[zz, c] + reach * o_recv[c].reshape(HD, PAIR)).astype(BF16)

        def prefix_out(zz):
            p_send[c, zz] = prefix(zz)
            send_prefix(c, zz, z).start()

        loop_z(prefix_out)
        p_recv[c, z] = prefix(z)

    upto = -(1 + lax.broadcasted_iota(jnp.int32, (tok, PAIR), 0)).astype(F32)

    def finish(c):
        before = jnp.where(z == 0, before_line(), last_of((me + n - 1) % n))
        gaps = jnp.where(doc[...] == before, upto, FAR)

        loop_z(lambda zz: send_prefix(c, z, zz).wait_recv())
        total = sumsq[...]
        for zz in range(nz):
            pair = zz * chunks + c
            state = p_recv[c, zz]
            wide = jnp.concatenate([state * keep_low, state * keep_high], 0)
            inter = dot(q_ref[:, pair * PAIR:(pair + 1) * PAIR], wide, PLAIN)
            value = raw[:, pair * PAIR:(pair + 1) * PAIR] + inter * jnp.exp(gaps * pair_rate(pair))
            raw[:, pair * PAIR:(pair + 1) * PAIR] = value
            total = total + value * value
        sumsq[...] = total

    stages = ((scan_line, 0.0), (scan_lines, 4.3), (carry_lines, 6.3), (prefixes, 10.6))
    events = sorted((2.8 * c + lag, i, c) for i, (_, lag) in enumerate(stages) for c in range(chunks))
    share = -(-pairs // max(1, len(events) - 4))
    share += share % 2
    done = 0
    for place, (_, i, c) in enumerate(events):
        want = min(pairs, share * (place + 1))
        if want > done:
            over_pairs(done, want, 2, intra)
            done = want
        stages[i][0](c)
    for c in range(chunks):
        finish(c)

    width = n * HD
    mean = jnp.sum(sumsq[...], axis=1, keepdims=True) * (1.0 / width)
    scale = jnp.broadcast_to(lax.rsqrt(mean + 1e-6), (tok, PAIR))

    def write(pair):
        columns = pair_columns(pair)
        out_ref[:, columns] = (raw[:, columns] * scale * gain_ref[0:1, columns]).astype(BF16)
    over_pairs(0, pairs, 4, write)

    loop_z(lambda zz: info_z(x * nz + zz, me).wait_send())
    loop_x(lambda xx: info_x(xx, x).wait_send())
    for c in range(chunks):
        loop_z(lambda zz: send_state(c, zz, z).wait_send())
        loop_x(lambda xx: send_total(c, xx, x).wait_send())
        send_slice(c, 1).wait_send()
        send_slice(c, 2).wait_send()
        loop_x(lambda xx: send_carry(c, xx, x).wait_send())
        loop_z(lambda zz: send_prefix(c, zz, z).wait_send())


def solution(mesh, nz=None):
    nctx, n = mesh.shape["ctx"], mesh.shape["uly"]
    nz = nz or math.isqrt(n)
    nx = n // nz
    chunks, rx = nx // 2, HD // nx

    def local(queries, keys, values, doc_ids, decay_rate, norm_gain):
        tok, width = queries.shape
        vmem = pl.BlockSpec(memory_space=pltpu.VMEM)
        anywhere = pl.BlockSpec(memory_space=pltpu.HBM)
        sem = pltpu.SemaphoreType.DMA
        return pl.pallas_call(
            functools.partial(kernel, nx, nz, nctx, tok),
            out_shape=jax.ShapeDtypeStruct((tok, width), BF16),
            in_specs=[anywhere] * 5 + [pl.BlockSpec(memory_space=pltpu.SMEM)],
            out_specs=vmem,
            scratch_shapes=[
                pltpu.VMEM((1, tok), jnp.int32),
                pltpu.VMEM((1, width), F32),
                pltpu.VMEM((tok, width), BF16),
                pltpu.VMEM((tok, width), BF16),
                pltpu.VMEM((tok, width), BF16),
                pltpu.VMEM((n // 2, PAIR, tok), F32),
                pltpu.VMEM((n // 2, 2 * tok, tok), F32),
                pltpu.VMEM((n, 2, PAIR), F32),
                pltpu.VMEM((tok, tok), F32),
                pltpu.VMEM((tok, PAIR), F32),
                pltpu.VMEM((tok, width), F32),
                pltpu.VMEM((tok, PAIR), F32),
                pltpu.VMEM((chunks, nz, HD, PAIR), BF16),
                pltpu.VMEM((chunks, nz, HD, PAIR), BF16),
                pltpu.VMEM((nz + 1, chunks, HD, PAIR), F32),
                pltpu.VMEM((chunks, nx, rx, PAIR), F32),
                pltpu.VMEM((chunks, nx, rx, PAIR), F32),
                pltpu.VMEM((chunks, rx + 8, PAIR), F32),
                pltpu.VMEM((chunks, rx + 8, PAIR), F32),
                pltpu.VMEM((chunks, rx + 8, PAIR), F32),
                pltpu.VMEM((chunks, nx, rx, PAIR), F32),
                pltpu.VMEM((chunks, nx, rx, PAIR), F32),
                pltpu.VMEM((chunks, nz, HD, PAIR), BF16),
                pltpu.VMEM((chunks, nz, HD, PAIR), BF16),
                pltpu.VMEM((8, PAIR), F32),
                sem((5,)),
                sem((nz,)), sem((nz,)), sem((nx,)), sem((nx,)),
                sem((chunks, nz)), sem((chunks, nz)),
                sem((chunks, nx)), sem((chunks, nx)),
                sem((chunks, 2)), sem((chunks, 2)),
                sem((chunks, nx)), sem((chunks, nx)),
                sem((chunks, nz)), sem((chunks, nz)),
            ],
            compiler_params=pltpu.CompilerParams(collective_id=0, has_side_effects=True,
                                                 vmem_limit_bytes=48 * 1024 * 1024),
        )(*(pltpu.with_memory_space_constraint(a, pltpu.HBM)
            for a in (queries, keys, values, doc_ids.reshape(1, tok), norm_gain.reshape(1, width))), decay_rate)

    rows = P(("ctx", "uly"), None)
    return jax.shard_map(local, mesh=mesh,
                         in_specs=(rows, rows, rows, P(("ctx", "uly")), P("uly"), P()),
                         out_specs=rows, check_vma=False)
```

```python
import functools
import math
import jax
import jax.numpy as jnp
from jax import lax
from jax.experimental import pallas as pl
from jax.experimental.pallas import tpu as pltpu
from jax.sharding import PartitionSpec as P

HD = 64
PAIR = 2 * HD
F32 = jnp.float32
BF16 = jnp.bfloat16
MESH = pl.DeviceIdType.MESH
CONTRACT_ROWS = (((0,), (0,)), ((), ()))
CONTRACT_LANES = (((1,), (1,)), ((), ()))
PLAIN = (((1,), (0,)), ((), ()))
FAR = -1e30


def dot(a, b, dims):
    return lax.dot_general(a, b, dims, preferred_element_type=F32)


def kernel(nx, nz, nctx, tok, q_hbm, k_hbm, v_hbm, ids_hbm, gain_hbm, rate_ref, out_ref,
           ids_ref, gain_ref, q_ref, k_ref, v_ref, k_turned, scores, info, negdiff, doc, raw, sumsq,
           s_send, s_recv, line, t_recv, ends, ends_recv, o_send, o_recv,
           p_send, p_recv,
           load_sem, iz_s, iz_r, ix_s, ix_r, s_s, s_r, t_s, t_r, ready, e_s, e_r, o_s, o_r, p_s, p_r):
    n = nx * nz
    chunks = nx // 2
    rx = HD // nx
    slab = nz * tok
    ctx = lax.axis_index("ctx")
    me = lax.axis_index("uly")
    x, z = me // nz, me % nz

    loads = [pltpu.make_async_copy(a, b, load_sem.at[i])
             for i, (a, b) in enumerate(((ids_hbm, ids_ref), (k_hbm, k_ref), (v_hbm, v_ref), (q_hbm, q_ref), (gain_hbm, gain_ref)))]
    barrier = pltpu.get_barrier_semaphore()

    def on_line(off):
        return (z + off) % nz

    def on_column(off):
        return (x + off) % nx

    def dev(xx, zz):
        return (ctx, xx * nz + zz)

    def greet_z(off, _):
        pl.semaphore_signal(barrier, inc=1, device_id=dev(x, on_line(off)), device_id_type=MESH)
        return 0

    def greet_x(off, _):
        pl.semaphore_signal(barrier, inc=1, device_id=dev(on_column(off), z), device_id_type=MESH)
        return 0

    lax.fori_loop(1, nz, greet_z, 0)
    lax.fori_loop(1, nx, greet_x, 0)
    for k in (1, 2):
        @pl.when(ctx + k < nctx)
        def _():
            def greet(xx, _):
                pl.semaphore_signal(barrier, inc=1, device_id=(ctx + k, xx * nz + z), device_id_type=MESH)
                return 0
            lax.fori_loop(0, nx, greet, 0)
    for load in loads:
        load.start()

    loads[0].wait()
    ids = ids_ref[...].astype(F32)
    last = jnp.max(ids, axis=1, keepdims=True)
    info[me] = jnp.where(lax.broadcasted_iota(jnp.int32, (2, PAIR), 0) < 1, jnp.full((2, PAIR), rate_ref[0], F32),
                         jnp.broadcast_to(last, (2, PAIR)))
    t_at = lax.broadcasted_iota(jnp.int32, (tok, tok), 0)
    s_at = lax.broadcasted_iota(jnp.int32, (tok, tok), 1)
    ids_all = jnp.broadcast_to(ids, (tok, tok))
    column = jnp.sum(jnp.where(t_at == s_at, ids_all, 0.0), axis=1, keepdims=True)
    negdiff[...] = jnp.where((t_at >= s_at) & (column == ids_all), (s_at - t_at).astype(F32), FAR)
    doc[...] = jnp.broadcast_to(column, (tok, PAIR))
    sumsq[...] = jnp.zeros_like(sumsq)
    for cond, slices in ((ctx == 0, 0), (ctx == 1, 1), (ctx >= 2, 2)):
        @pl.when(cond)
        def _():
            pl.semaphore_wait(barrier, nz + nx - 2 + slices * nx)

    def info_z(to, frm):
        return pltpu.make_async_remote_copy(info.at[frm], info.at[frm], iz_s.at[to % nz], iz_r.at[frm % nz],
                                            device_id=(ctx, to), device_id_type=MESH)

    def info_x(xto, xfrm):
        rows = info.at[pl.ds(xfrm * nz, nz)]
        return pltpu.make_async_remote_copy(rows, rows, ix_s.at[xto], ix_r.at[xfrm],
                                            device_id=dev(xto, z), device_id_type=MESH)

    def loop_z(body):
        def step(off, _):
            body(on_line(off))
            return 0
        lax.fori_loop(1, nz, step, 0)

    def loop_x(body):
        def step(off, _):
            body(on_column(off))
            return 0
        lax.fori_loop(1, nx, step, 0)

    def far_z(body):
        for off in sorted(range(1, nz), key=lambda o: -min(o, nz - o)):
            body(on_line(off))

    def every_x(body):
        for off in sorted(range(nx), key=lambda o: -min(o, nx - o)):
            body(on_column(off))

    def far_x(body):
        for off in sorted(range(1, nx), key=lambda o: -min(o, nx - o)):
            body(on_column(off))

    low = lax.broadcasted_iota(jnp.int32, (1, PAIR), 1) < HD
    mask_low = jnp.where(low, 1.0, 0.0)
    keep_low = mask_low.astype(BF16)
    keep_high = (1.0 - mask_low).astype(BF16)

    def pair_columns(pair):
        return pl.ds(pl.multiple_of(pair * PAIR, PAIR), PAIR)

    pairs = n // 2

    def over_pairs(first, end, width, body):
        def step(i, _):
            for j in range(width):
                body(first + i * width + j)
            return 0
        lax.fori_loop(0, (end - first) // width, step, 0)

    def turn(pair):
        k_turned[pair] = k_ref[:, pair_columns(pair)].astype(F32).T

    def score(pair):
        q2 = q_ref[:, pair_columns(pair)]
        qq = jnp.concatenate([q2 * keep_low, q2 * keep_high], 0)
        scores[pair] = dot(qq, k_ref[:, pair_columns(pair)], CONTRACT_LANES)

    far_z(lambda zz: info_z(x * nz + zz, me).start())
    for k in (1, 2):
        @pl.when(ctx >= k)
        def _():
            def welcome(xx, _):
                pl.semaphore_signal(ready.at[k - 1], inc=1, device_id=(ctx - k, xx * nz + z), device_id_type=MESH)
                return 0
            lax.fori_loop(0, nx, welcome, 0)
    loads[1].wait()
    over_pairs(0, pairs, 4, turn)
    loop_z(lambda zz: info_z(me, x * nz + zz).wait_recv())
    far_x(lambda xx: info_x(xx, x).start())
    for load in loads[2:]:
        load.wait()
    over_pairs(0, pairs, 4, score)
    loop_x(lambda xx: info_x(x, xx).wait_recv())

    def send_ends(k):
        return pltpu.make_async_remote_copy(ends, ends_recv.at[k - 1], e_s.at[k - 1], e_r.at[k - 1],
                                            device_id=(ctx + k, me), device_id_type=MESH)

    def when_later(k, body):
        pl.when(ctx + k < nctx)(body)

    def when_earlier(k, body):
        pl.when(ctx >= k)(body)


    def pair_rate(pair):
        return jnp.where(low, info[2 * pair, 0:1, :], info[2 * pair + 1, 0:1, :])

    def last_of(j):
        return info[j, 1:2, :]

    def join(big, rows):
        return jnp.where(low, big[:rows], big[rows:])

    after = (tok - 1 - lax.broadcasted_iota(jnp.int32, (1, tok), 1)).astype(F32)
    after = jnp.where(ids == last, -after, FAR)

    def end_state(pair):
        turned = k_turned[pair]
        kp = jnp.concatenate([turned[:HD] * jnp.exp(after * info[2 * pair, 0:1, :tok]),
                              turned[HD:] * jnp.exp(after * info[2 * pair + 1, 0:1, :tok])], 0)
        vp = v_ref[:, pair_columns(pair)]
        high = kp.astype(BF16)
        rest = (kp - high.astype(F32)).astype(BF16)
        return join(dot(high, vp, PLAIN) + dot(rest, vp, PLAIN), HD).astype(BF16)

    def send_state(c, to, frm):
        return pltpu.make_async_remote_copy(s_send.at[c, to], s_recv.at[c, frm], s_s.at[c, to], s_r.at[c, frm],
                                            device_id=dev(x, to), device_id_type=MESH)

    ahead = 3

    def state_out(c):
        far_z(lambda zz: send_state(c, zz, z).start())

    for c in range(chunks):
        for off in range(1, nz):
            s_send[c, on_line(off)] = end_state(on_line(off) * chunks + c)
        if c < ahead:
            state_out(c)
        s_recv[c, z] = end_state(z * chunks + c)

    for xx in range(nx):
        ends[xx:xx + 1, :] = last_of(xx * nz + nz - 1)
    for k in (1, 2):
        @pl.when(ctx + k < nctx)
        def _():
            pl.semaphore_wait(ready.at[k - 1], nx)
            send_ends(k).start()

    def intra(pair):
        gaps = negdiff[...]
        weight = jnp.concatenate([jnp.exp(gaps * info[2 * pair, 0:1, :tok]),
                                  jnp.exp(gaps * info[2 * pair + 1, 0:1, :tok])], 0)
        probs = (scores[pair] * weight).astype(BF16)
        raw[:, pair_columns(pair)] = join(dot(probs, v_ref[:, pair_columns(pair)], PLAIN), tok)

    def send_total(c, k, to, frm):
        return pltpu.make_async_remote_copy(line.at[nz, c, pl.ds(pl.multiple_of(to * rx, rx), rx)],
                                            t_recv.at[c, k, frm], t_s.at[c, k, to], t_r.at[c, k, frm],
                                            device_id=(ctx + k, to * nz + z), device_id_type=MESH)

    def all_x(body):
        def step(xx, _):
            body(xx)
            return 0
        lax.fori_loop(0, nx, step, 0)

    def scan_line(c):
        decay = jnp.exp(-float(tok) * pair_rate(z * chunks + c))
        loop_z(lambda zz: send_state(c, z, zz).wait_recv())
        total = jnp.zeros((HD, PAIR), F32)
        for zz in range(nz):
            line[zz, c] = total
            state = s_recv[c, zz].astype(F32)
            if zz:
                here = last_of(x * nz + zz)
                state = state + jnp.where(here == last_of(x * nz + zz - 1), decay, 0.0) * total
            total = state
        line[nz, c] = total
        t_recv[c, 0, x] = line[nz, c, pl.ds(pl.multiple_of(x * rx, rx), rx)]
        far_x(lambda xx: send_total(c, 0, xx, x).start())
        for k in (1, 2):
            when_later(k, lambda: every_x(lambda xx: send_total(c, k, xx, x).start()))

    def send_carry(c, to, frm):
        return pltpu.make_async_remote_copy(o_send.at[c, to], o_recv.at[c, frm], o_s.at[c, to], o_r.at[c, frm],
                                            device_id=dev(to, z), device_id_type=MESH)

    def end_of(k, xx):
        return ends_recv[k - 1, xx:xx + 1, :] if k else last_of(xx * nz + nz - 1)

    def scan_lines(c):
        decay = jnp.exp(-float(slab) * pair_rate(z * chunks + c))
        if c == 0:
            for k in (1, 2):
                when_earlier(k, lambda: send_ends(k).wait_recv())
        for k in (2, 1):
            when_earlier(k, lambda: all_x(lambda xx: send_total(c, k, x, xx).wait_recv()))
        loop_x(lambda xx: send_total(c, 0, x, xx).wait_recv())
        carry, before = jnp.zeros((rx, PAIR), F32), None
        for k in (2, 1, 0):
            for xx in range(nx):
                here = end_of(k, xx)
                if k == 0:
                    o_send[c, xx] = carry
                    if xx == nx - 1:
                        break
                fresh = t_recv[c, k, xx]
                if k:
                    fresh = jnp.where(ctx >= k, fresh, 0.0)
                if before is not None:
                    fresh = fresh + jnp.where(here == before, decay, 0.0) * carry
                carry, before = fresh, here
        o_recv[c, x] = o_send[c, x]
        far_x(lambda xx: send_carry(c, xx, x).start())

    def send_prefix(c, to, frm):
        return pltpu.make_async_remote_copy(p_send.at[c, to], p_recv.at[c, frm], p_s.at[c, to], p_r.at[c, frm],
                                            device_id=dev(x, to), device_id_type=MESH)

    def before_line():
        slice_before = jnp.where(ctx >= 1, ends_recv[0, nx - 1:nx, :], -1.0)
        return jnp.where(x == 0, slice_before, last_of((me - z + n - 1) % n))

    def prefixes(c):
        rate = pair_rate(z * chunks + c)
        before = before_line()
        reach = []
        for zz in range(nz):
            far = jnp.exp(-float(tok * zz) * rate)
            reach.append(jnp.where(last_of(x * nz + zz - 1) == before, far, 0.0) if zz else far)
        loop_x(lambda xx: send_carry(c, x, xx).wait_recv())
        carry = o_recv[c].reshape(HD, PAIR)
        for zz in range(nz):
            p_send[c, zz] = (line[zz, c] + reach[zz] * carry).astype(BF16)
        far_z(lambda zz: send_prefix(c, zz, z).start())
        p_recv[c, z] = p_send[c, z]

    upto = -(1 + lax.broadcasted_iota(jnp.int32, (tok, PAIR), 0)).astype(F32)

    def finish(c):
        before = jnp.where(z == 0, before_line(), last_of((me + n - 1) % n))
        gaps = jnp.where(doc[...] == before, upto, FAR)

        loop_z(lambda zz: send_prefix(c, z, zz).wait_recv())
        total = sumsq[...]
        for zz in range(nz):
            pair = zz * chunks + c
            state = p_recv[c, zz]
            wide = jnp.concatenate([state * keep_low, state * keep_high], 0)
            inter = dot(q_ref[:, pair * PAIR:(pair + 1) * PAIR], wide, PLAIN)
            value = raw[:, pair * PAIR:(pair + 1) * PAIR] + inter * jnp.exp(gaps * pair_rate(pair))
            raw[:, pair * PAIR:(pair + 1) * PAIR] = value
            total = total + value * value
        sumsq[...] = total

    stages = ((scan_line, 0.0), (scan_lines, 6.0), (prefixes, 11.0))
    events = sorted((3.2 * c + lag, i, c) for i, (_, lag) in enumerate(stages) for c in range(chunks))
    done = 0
    for place, (_, i, c) in enumerate(events):
        want = (pairs * (5, 7, 8)[min(place, 2)]) // 16 * 2
        if want > done:
            over_pairs(done, want, 2, intra)
            done = want
        stages[i][0](c)
        if i == 0 and c + ahead < chunks:
            state_out(c + ahead)
    for c in range(chunks):
        finish(c)

    width = n * HD
    mean = jnp.sum(sumsq[...], axis=1, keepdims=True) * (1.0 / width)
    scale = jnp.broadcast_to(lax.rsqrt(mean + 1e-6), (tok, PAIR))

    def write(pair):
        columns = pair_columns(pair)
        out_ref[:, columns] = (raw[:, columns] * scale * gain_ref[0:1, columns]).astype(BF16)
    over_pairs(0, pairs, 4, write)

    loop_z(lambda zz: info_z(x * nz + zz, me).wait_send())
    loop_x(lambda xx: info_x(xx, x).wait_send())
    for k in (1, 2):
        when_later(k, lambda: send_ends(k).wait_send())
    for c in range(chunks):
        loop_z(lambda zz: send_state(c, zz, z).wait_send())
        for k in (1, 2):
            when_later(k, lambda: all_x(lambda xx: send_total(c, k, xx, x).wait_send()))
        loop_x(lambda xx: send_total(c, 0, xx, x).wait_send())
        loop_x(lambda xx: send_carry(c, xx, x).wait_send())
        loop_z(lambda zz: send_prefix(c, zz, z).wait_send())


def solution(mesh, nz=None):
    nctx, n = mesh.shape["ctx"], mesh.shape["uly"]
    nz = nz or math.isqrt(n)
    nx = n // nz
    chunks, rx = nx // 2, HD // nx

    def local(queries, keys, values, doc_ids, decay_rate, norm_gain):
        tok, width = queries.shape
        vmem = pl.BlockSpec(memory_space=pltpu.VMEM)
        anywhere = pl.BlockSpec(memory_space=pltpu.HBM)
        sem = pltpu.SemaphoreType.DMA
        return pl.pallas_call(
            functools.partial(kernel, nx, nz, nctx, tok),
            out_shape=jax.ShapeDtypeStruct((tok, width), BF16),
            in_specs=[anywhere] * 5 + [pl.BlockSpec(memory_space=pltpu.SMEM)],
            out_specs=vmem,
            scratch_shapes=[
                pltpu.VMEM((1, tok), jnp.int32),
                pltpu.VMEM((1, width), F32),
                pltpu.VMEM((tok, width), BF16),
                pltpu.VMEM((tok, width), BF16),
                pltpu.VMEM((tok, width), BF16),
                pltpu.VMEM((n // 2, PAIR, tok), F32),
                pltpu.VMEM((n // 2, 2 * tok, tok), F32),
                pltpu.VMEM((n, 2, PAIR), F32),
                pltpu.VMEM((tok, tok), F32),
                pltpu.VMEM((tok, PAIR), F32),
                pltpu.VMEM((tok, width), F32),
                pltpu.VMEM((tok, PAIR), F32),
                pltpu.VMEM((chunks, nz, HD, PAIR), BF16),
                pltpu.VMEM((chunks, nz, HD, PAIR), BF16),
                pltpu.VMEM((nz + 1, chunks, HD, PAIR), F32),
                pltpu.VMEM((chunks, 3, nx, rx, PAIR), F32),
                pltpu.VMEM((nx, PAIR), F32),
                pltpu.VMEM((2, nx, PAIR), F32),
                pltpu.VMEM((chunks, nx, rx, PAIR), F32),
                pltpu.VMEM((chunks, nx, rx, PAIR), F32),
                pltpu.VMEM((chunks, nz, HD, PAIR), BF16),
                pltpu.VMEM((chunks, nz, HD, PAIR), BF16),
                sem((5,)),
                sem((nz,)), sem((nz,)), sem((nx,)), sem((nx,)),
                sem((chunks, nz)), sem((chunks, nz)),
                sem((chunks, 3, nx)), sem((chunks, 3, nx)),
                pltpu.SemaphoreType.REGULAR((2,)), sem((2,)), sem((2,)),
                sem((chunks, nx)), sem((chunks, nx)),
                sem((chunks, nz)), sem((chunks, nz)),
            ],
            compiler_params=pltpu.CompilerParams(collective_id=0, has_side_effects=True,
                                                 vmem_limit_bytes=48 * 1024 * 1024),
        )(*(pltpu.with_memory_space_constraint(a, pltpu.HBM)
            for a in (queries, keys, values, doc_ids.reshape(1, tok), norm_gain.reshape(1, width))), decay_rate)

    rows = P(("ctx", "uly"), None)
    return jax.shard_map(local, mesh=mesh,
                         in_specs=(rows, rows, rows, P(("ctx", "uly")), P("uly"), P()),
                         out_specs=rows, check_vma=False)
```

```python
import functools
import math
import jax
import jax.numpy as jnp
from jax import lax
from jax.experimental import pallas as pl
from jax.experimental.pallas import tpu as pltpu
from jax.sharding import PartitionSpec as P

HD = 64
PAIR = 2 * HD
F32 = jnp.float32
BF16 = jnp.bfloat16
MESH = pl.DeviceIdType.MESH
CONTRACT_ROWS = (((0,), (0,)), ((), ()))
CONTRACT_LANES = (((1,), (1,)), ((), ()))
PLAIN = (((1,), (0,)), ((), ()))
FAR = -1e30


def dot(a, b, dims):
    return lax.dot_general(a, b, dims, preferred_element_type=F32)


def kernel(nx, nz, nctx, tok, q_hbm, k_hbm, v_hbm, ids_hbm, gain_hbm, rate_ref, out_ref,
           ids_ref, gain_ref, q_ref, k_ref, v_ref, k_turned, scores, info, negdiff, doc, raw, sumsq,
           s_send, s_recv, line, t_recv, ends, ends_recv, o_send, o_recv,
           p_send, p_recv,
           load_sem, iz_s, iz_r, ix_s, ix_r, s_s, s_r, t_s, t_r, ready, e_s, e_r, o_s, o_r, p_s, p_r):
    n = nx * nz
    chunks = nx // 2
    rx = HD // nx
    slab = nz * tok
    ctx = lax.axis_index("ctx")
    me = lax.axis_index("uly")
    x, z = me // nz, me % nz

    loads = [pltpu.make_async_copy(a, b, load_sem.at[i])
             for i, (a, b) in enumerate(((ids_hbm, ids_ref), (k_hbm, k_ref), (v_hbm, v_ref), (q_hbm, q_ref), (gain_hbm, gain_ref)))]
    barrier = pltpu.get_barrier_semaphore()

    def on_line(off):
        return (z + off) % nz

    def on_column(off):
        return (x + off) % nx

    def dev(xx, zz):
        return (ctx, xx * nz + zz)

    def greet_z(off, _):
        pl.semaphore_signal(barrier, inc=1, device_id=dev(x, on_line(off)), device_id_type=MESH)
        return 0

    def greet_x(off, _):
        pl.semaphore_signal(barrier, inc=1, device_id=dev(on_column(off), z), device_id_type=MESH)
        return 0

    lax.fori_loop(1, nz, greet_z, 0)
    lax.fori_loop(1, nx, greet_x, 0)
    for k in (1, 2):
        @pl.when(ctx + k < nctx)
        def _():
            def greet(xx, _):
                pl.semaphore_signal(barrier, inc=1, device_id=(ctx + k, xx * nz + z), device_id_type=MESH)
                return 0
            lax.fori_loop(0, nx, greet, 0)
    for load in loads:
        load.start()

    loads[0].wait()
    ids = ids_ref[...].astype(F32)
    last = jnp.max(ids, axis=1, keepdims=True)
    info[me] = jnp.where(lax.broadcasted_iota(jnp.int32, (2, PAIR), 0) < 1, jnp.full((2, PAIR), rate_ref[0], F32),
                         jnp.broadcast_to(last, (2, PAIR)))
    t_at = lax.broadcasted_iota(jnp.int32, (tok, tok), 0)
    s_at = lax.broadcasted_iota(jnp.int32, (tok, tok), 1)
    ids_all = jnp.broadcast_to(ids, (tok, tok))
    column = jnp.sum(jnp.where(t_at == s_at, ids_all, 0.0), axis=1, keepdims=True)
    negdiff[...] = jnp.where((t_at >= s_at) & (column == ids_all), (s_at - t_at).astype(F32), FAR)
    doc[...] = jnp.broadcast_to(column, (tok, PAIR))
    sumsq[...] = jnp.zeros_like(sumsq)
    for cond, slices in ((ctx == 0, 0), (ctx == 1, 1), (ctx >= 2, 2)):
        @pl.when(cond)
        def _():
            pl.semaphore_wait(barrier, nz + nx - 2 + slices * nx)

    def info_z(to, frm):
        return pltpu.make_async_remote_copy(info.at[frm], info.at[frm], iz_s.at[to % nz], iz_r.at[frm % nz],
                                            device_id=(ctx, to), device_id_type=MESH)

    def info_x(xto, xfrm):
        rows = info.at[pl.ds(xfrm * nz, nz)]
        return pltpu.make_async_remote_copy(rows, rows, ix_s.at[xto], ix_r.at[xfrm],
                                            device_id=dev(xto, z), device_id_type=MESH)

    def loop_z(body):
        def step(off, _):
            body(on_line(off))
            return 0
        lax.fori_loop(1, nz, step, 0)

    def loop_x(body):
        def step(off, _):
            body(on_column(off))
            return 0
        lax.fori_loop(1, nx, step, 0)

    def far_z(body):
        for off in sorted(range(1, nz), key=lambda o: -min(o, nz - o)):
            body(on_line(off))

    def far_x(body):
        for off in sorted(range(1, nx), key=lambda o: -min(o, nx - o)):
            body(on_column(off))

    low = lax.broadcasted_iota(jnp.int32, (1, PAIR), 1) < HD
    mask_low = jnp.where(low, 1.0, 0.0)
    keep_low = mask_low.astype(BF16)
    keep_high = (1.0 - mask_low).astype(BF16)

    def pair_columns(pair):
        return pl.ds(pl.multiple_of(pair * PAIR, PAIR), PAIR)

    pairs = n // 2

    def over_pairs(first, end, width, body):
        def step(i, _):
            for j in range(width):
                body(first + i * width + j)
            return 0
        lax.fori_loop(0, (end - first) // width, step, 0)

    def turn(pair):
        k_turned[pair] = k_ref[:, pair_columns(pair)].astype(F32).T

    def score(pair):
        q2 = q_ref[:, pair_columns(pair)]
        qq = jnp.concatenate([q2 * keep_low, q2 * keep_high], 0)
        scores[pair] = dot(qq, k_ref[:, pair_columns(pair)], CONTRACT_LANES)

    far_z(lambda zz: info_z(x * nz + zz, me).start())
    for k in (1, 2):
        @pl.when(ctx >= k)
        def _():
            def welcome(xx, _):
                pl.semaphore_signal(ready.at[k - 1], inc=1, device_id=(ctx - k, xx * nz + z), device_id_type=MESH)
                return 0
            lax.fori_loop(0, nx, welcome, 0)
    loads[1].wait()
    over_pairs(0, pairs, 4, turn)
    loop_z(lambda zz: info_z(me, x * nz + zz).wait_recv())
    far_x(lambda xx: info_x(xx, x).start())
    for load in loads[2:]:
        load.wait()
    over_pairs(0, pairs, 4, score)
    loop_x(lambda xx: info_x(x, xx).wait_recv())

    def send_ends(k):
        return pltpu.make_async_remote_copy(ends, ends_recv.at[k - 1], e_s.at[k - 1], e_r.at[k - 1],
                                            device_id=(ctx + k, me), device_id_type=MESH)

    def when_later(k, body):
        pl.when(ctx + k < nctx)(body)

    def when_earlier(k, body):
        pl.when(ctx >= k)(body)


    def pair_rate(pair):
        return jnp.where(low, info[2 * pair, 0:1, :], info[2 * pair + 1, 0:1, :])

    def last_of(j):
        return info[j, 1:2, :]

    def join(big, rows):
        return jnp.where(low, big[:rows], big[rows:])

    after = (tok - 1 - lax.broadcasted_iota(jnp.int32, (1, tok), 1)).astype(F32)
    after = jnp.where(ids == last, -after, FAR)

    def end_state(pair):
        turned = k_turned[pair]
        kp = jnp.concatenate([turned[:HD] * jnp.exp(after * info[2 * pair, 0:1, :tok]),
                              turned[HD:] * jnp.exp(after * info[2 * pair + 1, 0:1, :tok])], 0)
        vp = v_ref[:, pair_columns(pair)]
        high = kp.astype(BF16)
        rest = (kp - high.astype(F32)).astype(BF16)
        return join(dot(high, vp, PLAIN) + dot(rest, vp, PLAIN), HD).astype(BF16)

    def send_state(c, to, frm):
        return pltpu.make_async_remote_copy(s_send.at[c, to], s_recv.at[c, frm], s_s.at[c, to], s_r.at[c, frm],
                                            device_id=dev(x, to), device_id_type=MESH)

    ahead = 2

    def state_out(c):
        far_z(lambda zz: send_state(c, zz, z).start())

    for c in range(chunks):
        for off in range(1, nz):
            s_send[c, on_line(off)] = end_state(on_line(off) * chunks + c)
        if c < ahead:
            state_out(c)
        s_recv[c, z] = end_state(z * chunks + c)

    for xx in range(nx):
        ends[xx:xx + 1, :] = last_of(xx * nz + nz - 1)
    for k in (1, 2):
        @pl.when(ctx + k < nctx)
        def _():
            pl.semaphore_wait(ready.at[k - 1], nx)
            send_ends(k).start()

    def intra(pair):
        gaps = negdiff[...]
        weight = jnp.concatenate([jnp.exp(gaps * info[2 * pair, 0:1, :tok]),
                                  jnp.exp(gaps * info[2 * pair + 1, 0:1, :tok])], 0)
        probs = (scores[pair] * weight).astype(BF16)
        raw[:, pair_columns(pair)] = join(dot(probs, v_ref[:, pair_columns(pair)], PLAIN), tok)

    def send_total(c, k, to, frm):
        return pltpu.make_async_remote_copy(line.at[nz, c, pl.ds(pl.multiple_of(to * rx, rx), rx)],
                                            t_recv.at[c, k, frm], t_s.at[c, k, to], t_r.at[c, k, frm],
                                            device_id=(ctx + k, to * nz + z), device_id_type=MESH)

    def all_x(body):
        def step(xx, _):
            body(xx)
            return 0
        lax.fori_loop(0, nx, step, 0)

    def scan_line(c):
        decay = jnp.exp(-float(tok) * pair_rate(z * chunks + c))
        loop_z(lambda zz: send_state(c, z, zz).wait_recv())
        total = jnp.zeros((HD, PAIR), F32)
        for zz in range(nz):
            line[zz, c] = total
            state = s_recv[c, zz].astype(F32)
            if zz:
                here = last_of(x * nz + zz)
                state = state + jnp.where(here == last_of(x * nz + zz - 1), decay, 0.0) * total
            total = state
        line[nz, c] = total
        t_recv[c, 0, x] = line[nz, c, pl.ds(pl.multiple_of(x * rx, rx), rx)]
        for k in (2, 1):
            when_later(k, lambda: all_x(lambda xx: send_total(c, k, xx, x).start()))
        far_x(lambda xx: send_total(c, 0, xx, x).start())

    def send_carry(c, to, frm):
        return pltpu.make_async_remote_copy(o_send.at[c, to], o_recv.at[c, frm], o_s.at[c, to], o_r.at[c, frm],
                                            device_id=dev(to, z), device_id_type=MESH)

    def end_of(k, xx):
        return ends_recv[k - 1, xx:xx + 1, :] if k else last_of(xx * nz + nz - 1)

    def scan_lines(c):
        decay = jnp.exp(-float(slab) * pair_rate(z * chunks + c))
        if c == 0:
            for k in (1, 2):
                when_earlier(k, lambda: send_ends(k).wait_recv())
        for k in (2, 1):
            when_earlier(k, lambda: all_x(lambda xx: send_total(c, k, x, xx).wait_recv()))
        loop_x(lambda xx: send_total(c, 0, x, xx).wait_recv())
        carry, before = jnp.zeros((rx, PAIR), F32), None
        for k in (2, 1, 0):
            for xx in range(nx):
                here = end_of(k, xx)
                if k == 0:
                    o_send[c, xx] = carry
                    if xx == nx - 1:
                        break
                fresh = t_recv[c, k, xx]
                if k:
                    fresh = jnp.where(ctx >= k, fresh, 0.0)
                if before is not None:
                    fresh = fresh + jnp.where(here == before, decay, 0.0) * carry
                carry, before = fresh, here
        o_recv[c, x] = o_send[c, x]
        far_x(lambda xx: send_carry(c, xx, x).start())

    def send_prefix(c, to, frm):
        return pltpu.make_async_remote_copy(p_send.at[c, to], p_recv.at[c, frm], p_s.at[c, to], p_r.at[c, frm],
                                            device_id=dev(x, to), device_id_type=MESH)

    def before_line():
        slice_before = jnp.where(ctx >= 1, ends_recv[0, nx - 1:nx, :], -1.0)
        return jnp.where(x == 0, slice_before, last_of((me - z + n - 1) % n))

    def prefixes(c):
        rate = pair_rate(z * chunks + c)
        before = before_line()
        reach = []
        for zz in range(nz):
            far = jnp.exp(-float(tok * zz) * rate)
            reach.append(jnp.where(last_of(x * nz + zz - 1) == before, far, 0.0) if zz else far)
        loop_x(lambda xx: send_carry(c, x, xx).wait_recv())
        carry = o_recv[c].reshape(HD, PAIR)
        for zz in range(nz):
            p_send[c, zz] = (line[zz, c] + reach[zz] * carry).astype(BF16)
        far_z(lambda zz: send_prefix(c, zz, z).start())
        p_recv[c, z] = p_send[c, z]

    upto = -(1 + lax.broadcasted_iota(jnp.int32, (tok, PAIR), 0)).astype(F32)

    def finish(c):
        before = jnp.where(z == 0, before_line(), last_of((me + n - 1) % n))
        gaps = jnp.where(doc[...] == before, upto, FAR)

        loop_z(lambda zz: send_prefix(c, z, zz).wait_recv())
        total = sumsq[...]
        for zz in range(nz):
            pair = zz * chunks + c
            state = p_recv[c, zz]
            wide = jnp.concatenate([state * keep_low, state * keep_high], 0)
            inter = dot(q_ref[:, pair * PAIR:(pair + 1) * PAIR], wide, PLAIN)
            value = raw[:, pair * PAIR:(pair + 1) * PAIR] + inter * jnp.exp(gaps * pair_rate(pair))
            raw[:, pair * PAIR:(pair + 1) * PAIR] = value
            total = total + value * value
        sumsq[...] = total

    stages = ((scan_line, 0.0), (scan_lines, 6.0), (prefixes, 11.0))
    events = sorted((3.2 * c + lag, i, c) for i, (_, lag) in enumerate(stages) for c in range(chunks))
    done = 0
    for place, (_, i, c) in enumerate(events):
        want = (pairs * (5, 7, 8)[min(place, 2)]) // 16 * 2
        if want > done:
            over_pairs(done, want, 2, intra)
            done = want
        stages[i][0](c)
        if i == 0 and c + ahead < chunks:
            state_out(c + ahead)
    for c in range(chunks):
        finish(c)

    width = n * HD
    mean = jnp.sum(sumsq[...], axis=1, keepdims=True) * (1.0 / width)
    scale = jnp.broadcast_to(lax.rsqrt(mean + 1e-6), (tok, PAIR))

    def write(pair):
        columns = pair_columns(pair)
        out_ref[:, columns] = (raw[:, columns] * scale * gain_ref[0:1, columns]).astype(BF16)
    over_pairs(0, pairs, 4, write)

    loop_z(lambda zz: info_z(x * nz + zz, me).wait_send())
    loop_x(lambda xx: info_x(xx, x).wait_send())
    for k in (1, 2):
        when_later(k, lambda: send_ends(k).wait_send())
    for c in range(chunks):
        loop_z(lambda zz: send_state(c, zz, z).wait_send())
        for k in (1, 2):
            when_later(k, lambda: all_x(lambda xx: send_total(c, k, xx, x).wait_send()))
        loop_x(lambda xx: send_total(c, 0, xx, x).wait_send())
        loop_x(lambda xx: send_carry(c, xx, x).wait_send())
        loop_z(lambda zz: send_prefix(c, zz, z).wait_send())


def solution(mesh, nz=None):
    nctx, n = mesh.shape["ctx"], mesh.shape["uly"]
    nz = nz or math.isqrt(n)
    nx = n // nz
    chunks, rx = nx // 2, HD // nx

    def local(queries, keys, values, doc_ids, decay_rate, norm_gain):
        tok, width = queries.shape
        vmem = pl.BlockSpec(memory_space=pltpu.VMEM)
        anywhere = pl.BlockSpec(memory_space=pltpu.HBM)
        sem = pltpu.SemaphoreType.DMA
        return pl.pallas_call(
            functools.partial(kernel, nx, nz, nctx, tok),
            out_shape=jax.ShapeDtypeStruct((tok, width), BF16),
            in_specs=[anywhere] * 5 + [pl.BlockSpec(memory_space=pltpu.SMEM)],
            out_specs=vmem,
            scratch_shapes=[
                pltpu.VMEM((1, tok), jnp.int32),
                pltpu.VMEM((1, width), F32),
                pltpu.VMEM((tok, width), BF16),
                pltpu.VMEM((tok, width), BF16),
                pltpu.VMEM((tok, width), BF16),
                pltpu.VMEM((n // 2, PAIR, tok), F32),
                pltpu.VMEM((n // 2, 2 * tok, tok), F32),
                pltpu.VMEM((n, 2, PAIR), F32),
                pltpu.VMEM((tok, tok), F32),
                pltpu.VMEM((tok, PAIR), F32),
                pltpu.VMEM((tok, width), F32),
                pltpu.VMEM((tok, PAIR), F32),
                pltpu.VMEM((chunks, nz, HD, PAIR), BF16),
                pltpu.VMEM((chunks, nz, HD, PAIR), BF16),
                pltpu.VMEM((nz + 1, chunks, HD, PAIR), F32),
                pltpu.VMEM((chunks, 3, nx, rx, PAIR), F32),
                pltpu.VMEM((nx, PAIR), F32),
                pltpu.VMEM((2, nx, PAIR), F32),
                pltpu.VMEM((chunks, nx, rx, PAIR), F32),
                pltpu.VMEM((chunks, nx, rx, PAIR), F32),
                pltpu.VMEM((chunks, nz, HD, PAIR), BF16),
                pltpu.VMEM((chunks, nz, HD, PAIR), BF16),
                sem((5,)),
                sem((nz,)), sem((nz,)), sem((nx,)), sem((nx,)),
                sem((chunks, nz)), sem((chunks, nz)),
                sem((chunks, 3, nx)), sem((chunks, 3, nx)),
                pltpu.SemaphoreType.REGULAR((2,)), sem((2,)), sem((2,)),
                sem((chunks, nx)), sem((chunks, nx)),
                sem((chunks, nz)), sem((chunks, nz)),
            ],
            compiler_params=pltpu.CompilerParams(collective_id=0, has_side_effects=True,
                                                 vmem_limit_bytes=48 * 1024 * 1024),
        )(*(pltpu.with_memory_space_constraint(a, pltpu.HBM)
            for a in (queries, keys, values, doc_ids.reshape(1, tok), norm_gain.reshape(1, width))), decay_rate)

    rows = P(("ctx", "uly"), None)
    return jax.shard_map(local, mesh=mesh,
                         in_specs=(rows, rows, rows, P(("ctx", "uly")), P("uly"), P()),
                         out_specs=rows, check_vma=False)
```
